32 devices in a mesh: rep: 2 (over y), seq: 4 (over z), ch: 4 (over x, core).
Axes of the slice: x: 2, y: 2, z: 4, core: 2. Of those that a mesh axis runs over, the one named last changes fastest.
Arguments:
- key_proj: bfloat16 [4096, 4096], P(('rep', 'seq'), 'ch'), parts along dimension 0, may hold values from -6 to 6
- value_proj: bfloat16 [4096, 4096], P(('rep', 'seq'), 'ch'), parts along dimension 0, may hold values from -6 to 6
- query_proj: bfloat16 [4096, 4096], P(('rep', 'seq'), 'ch'), parts along dimension 0, may hold values from -6 to 6
- filters: bfloat16 [256, 2048], P('ch', 'seq'), may hold values from -3 to 3
- sources: int32 [8], P('rep'), parts along dimension 0, may hold values from 0 to 15, as said below
- owner: int32 [32], P('rep'), parts along dimension 0, may hold values from 0 to 3, as said below
Outputs:
- conv_out: bfloat16 [4096, 4096], P(('rep', 'seq'), 'ch'), parts along dimension 0
The draws below stay inside these ranges and needn't reach their ends.
There are 2 independent parts, one for each index of `rep`. The reference program is written for one: setup_inputs(seed, part) draws one part's arguments, and reference() takes and returns one part's arrays. A program takes and returns all parts, laid end to end along the dimension named above; an argument that names none is the same for every part. Nothing has to cross between parts.
Inputs may be any that keep to these rules, and one draw needn't show every extreme that they name: `sources`: four distinct stretch numbers in increasing order; the first is 0 and the last 15. owner[k] is the index along seq of the shard holding stretch k; every shard holds exactly 4 stretches, stored one after another in increasing stretch number.
All inputs are finite; a program needn't handle non-finite values.
Results may differ from the reference program's by a relative error of at most 0.0049.
Values may be sent and summed in bfloat16 or wider, within the bound.
A program may use at most 64 MiB of HBM per device.

```python
import math
import jax
import jax.numpy as jnp
from jax import lax

D = 4096
GROUP_CH = 16
FILTER_GROUPS = 256
STRETCH = 128
WIN = 4
CH_DEV = 4
NCH = 16
SEQUENCE_LENGTH = 2048


def channel_offsets(key):
    sign_key, size_key = jax.random.split(jax.random.fold_in(key, 31))
    signs = jnp.where(jax.random.uniform(sign_key, (D,)) < 0.5, -1.0, 1.0)
    return signs * jax.random.uniform(size_key, (D,), minval=0.7, maxval=1.3)


def stretch_levels(key, salt):
    level_key = jax.random.fold_in(key, salt)
    return jnp.exp(jax.random.uniform(level_key, (NCH, 1, 1), minval=-4.0, maxval=1.0))


def draw_key_proj(key, part):
    offsets = channel_offsets(key)
    levels = stretch_levels(key, 41)
    noise_key = jax.random.fold_in(key, 43)
    noise = jax.random.normal(noise_key, (NCH, STRETCH, D))
    rows = jnp.clip(levels * (noise + offsets[None, None, :]), -6.0, 6.0)
    return rows.reshape(SEQUENCE_LENGTH, D).astype(jnp.bfloat16)


def draw_value_proj(key, part):
    offsets = channel_offsets(key)
    levels = stretch_levels(key, 47)
    noise_key = jax.random.fold_in(key, 53)
    noise = jax.random.normal(noise_key, (NCH, STRETCH, D))
    rows = jnp.clip(levels * (noise + offsets[None, None, :]), -6.0, 6.0)
    return rows.reshape(SEQUENCE_LENGTH, D).astype(jnp.bfloat16)


def draw_filters(key, part):
    first, second, third, fourth_random_key, fifth = jax.random.split(jax.random.fold_in(key, 7), 5)
    lag_dimension = jnp.arange(SEQUENCE_LENGTH, dtype=jnp.float32)
    quick = float(min(40, max(4, STRETCH // 2)))
    slow_share = 0.5
    slow_flag = jax.random.uniform(first, (FILTER_GROUPS, 1)) < slow_share
    fast_log = jax.random.uniform(second, (FILTER_GROUPS, 1), minval=math.log(quick), maxval=math.log(float(SEQUENCE_LENGTH)))
    slow_log = jax.random.uniform(third, (FILTER_GROUPS, 1), minval=math.log(float(SEQUENCE_LENGTH)), maxval=math.log(50.0 * SEQUENCE_LENGTH))
    decay_len = jnp.exp(jnp.where(slow_flag, slow_log, fast_log))
    spike_lag_offset = jax.random.randint(fourth_random_key, (FILTER_GROUPS, 3, 1), 1, SEQUENCE_LENGTH).astype(jnp.float32)
    retained_fraction = jax.random.uniform(fifth, (FILTER_GROUPS, 3, 1), minval=0.5, maxval=0.8)
    discarded_mask = jnp.prod(jnp.where(lag_dimension[None, None, :] >= spike_lag_offset, retained_fraction, 1.0), axis=1)
    scale = 1.0 / jnp.sqrt(jnp.minimum(decay_len, float(STRETCH)))
    noise_key = jax.random.fold_in(key, 13)
    rough = jnp.clip(jax.random.normal(noise_key, (FILTER_GROUPS, SEQUENCE_LENGTH)), -6.0, 6.0)
    near_part = rough * jnp.exp(-lag_dimension[None, :] / decay_len) * discarded_mask * scale
    sign_key = jax.random.fold_in(key, 17)
    tail_sign = jnp.where(jax.random.uniform(sign_key, (FILTER_GROUPS, 1)) < 0.5, -1.0, 1.0)
    tail_rough = 0.25 + 1.5 * jax.random.uniform(jax.random.fold_in(key, 19), (FILTER_GROUPS, SEQUENCE_LENGTH))
    tail_part = 0.015 * scale * tail_sign * tail_rough * jnp.exp(-lag_dimension[None, :] / (2.0 * SEQUENCE_LENGTH))
    return (near_part + tail_part).astype(jnp.bfloat16)


def draw_sources(key, part):
    inner = jax.random.permutation(jax.random.fold_in(key, 11), NCH - 2)[:2] + 1
    lower = jnp.minimum(inner[0], inner[1])
    upper = jnp.maximum(inner[0], inner[1])
    return jnp.stack([jnp.int32(0), lower.astype(jnp.int32), upper.astype(jnp.int32), jnp.int32(NCH - 1)]).astype(jnp.int32)


def draw_owner(key, part):
    shuffled = jax.random.permutation(jax.random.fold_in(key, 23), NCH)
    return (shuffled // CH_DEV).astype(jnp.int32)


def level_of(rng, dims, shards, smallest, largest):
    def one(dim, parts):
        draws = jax.random.uniform(jax.random.fold_in(jax.random.fold_in(rng, 6), dim), (parts,), jnp.float32, smallest / len(shards), largest / len(shards))
        return jnp.repeat(jnp.exp(draws), dims[dim] // parts).reshape((-1,) + (1,) * (len(dims) - dim - 1))

    factor_of = one(*shards[0])
    for cut in shards[1:]:
        factor_of = factor_of * one(*cut)
    return factor_of


def bell_draw(stream_key, extent, deviation, bound, shards=(), kind=jnp.bfloat16):
    array = deviation * jax.random.normal(stream_key, extent, jnp.float32)
    if shards:
        array = array * level_of(stream_key, extent, shards, -0.22, 0.18)
    return jnp.clip(array, -bound, bound).astype(kind)


def setup_inputs(seed: int = 0, part: int = 0) -> dict:
    seeds = jax.random.split(jax.random.key(seed), 7)
    part_keys = jax.random.split(jax.random.fold_in(seeds[6], part), 7)
    return {
        "key_proj": draw_key_proj(jax.random.fold_in(jax.random.fold_in(seeds[6], part), 71), part),
        "value_proj": draw_value_proj(jax.random.fold_in(jax.random.fold_in(seeds[6], part), 71), part),
        "query_proj": bell_draw(part_keys[2], (SEQUENCE_LENGTH, D), 1.0, 6.0, ((0, 4), (1, 4))),
        "filters": draw_filters(jax.random.fold_in(seeds[6], 71), part),
        "sources": draw_sources(jax.random.fold_in(jax.random.fold_in(seeds[6], part), 71), part),
        "owner": draw_owner(jax.random.fold_in(jax.random.fold_in(seeds[6], part), 71), part),
    }


def reference(key_proj, value_proj, query_proj, filters, sources, owner):
    stretch_total = owner.shape[0]
    channels = key_proj.shape[1]
    group_count = channels // GROUP_CH
    numbers = jnp.arange(stretch_total, dtype=jnp.int32)
    same_owner = (owner[:, None] == owner[None, :]).astype(jnp.int32)
    earlier = (numbers[None, :] < numbers[:, None]).astype(jnp.int32)
    position = (owner * CH_DEV + jnp.sum(same_owner * earlier, axis=1)).astype(jnp.int32)
    stretch_at = jnp.sum((position[None, :] == numbers[:, None]).astype(jnp.int32) * numbers[None, :], axis=1).astype(jnp.int32)
    source_at = jnp.sum((sources[:, None] == numbers[None, :]).astype(jnp.int32) * position[None, :], axis=1).astype(jnp.int32)
    gated = (key_proj.astype(jnp.float32) * value_proj.astype(jnp.float32)).astype(jnp.bfloat16)
    blocks = gated.reshape(stretch_total, STRETCH, group_count, GROUP_CH)
    window = jnp.take(blocks, source_at, axis=0).astype(jnp.float32)
    padded = jnp.concatenate([jnp.zeros((group_count, STRETCH), jnp.float32), filters.astype(jnp.float32)], axis=1)
    offsets = (STRETCH + jnp.arange(STRETCH, dtype=jnp.int32)[:, None] - jnp.arange(STRETCH, dtype=jnp.int32)[None, :]).astype(jnp.int32)

    def one_block(stored):
        target = stretch_at[stored]
        summed = jnp.zeros((STRETCH, group_count, GROUP_CH), jnp.float32)
        for window_slot in range(WIN):
            lag_block = target - sources[window_slot]
            lag_start = (jnp.maximum(lag_block, 0) * STRETCH).astype(jnp.int32)
            lag_span = lax.dynamic_slice_in_dim(padded, lag_start, 2 * STRETCH, 1)
            toeplitz = jnp.take(lag_span, offsets, axis=1)
            term = jnp.einsum("gij,jgc->igc", toeplitz, window[window_slot], precision=lax.Precision.HIGHEST)
            summed = summed + jnp.where(lag_block >= 0, term, 0.0)
        gate_rows = lax.dynamic_slice_in_dim(query_proj, (stored * STRETCH).astype(jnp.int32), STRETCH, 0).astype(jnp.float32)
        return (gate_rows * summed.reshape(STRETCH, channels)).astype(jnp.bfloat16)

    result = lax.map(one_block, numbers)
    return result.reshape(stretch_total * STRETCH, channels)
```

```python
import jax
import jax.numpy as jnp
from jax import lax
from jax.experimental import pallas as pl
from jax.experimental.pallas import tpu as pltpu
from jax.sharding import PartitionSpec as P

GROUP_CH = 16
STRETCH = 128
WIN = 4
PIECE = 16
OCT = 8
F32 = jnp.float32
BF16 = jnp.bfloat16


def lane_block(rows):
    return lax.broadcasted_iota(jnp.int32, (rows, 128), 1) // PIECE


def block_transpose(parts):
    parts = list(parts)
    block = lane_block(parts[0].shape[0])
    for step in (1, 2, 4):
        keep = (block & step) == 0
        for p in range(OCT):
            if p & step:
                continue
            low, high = parts[p], parts[p + step]
            parts[p] = jnp.where(keep, low, pltpu.roll(high, PIECE * step, 1))
            parts[p + step] = jnp.where(keep, pltpu.roll(low, 128 - PIECE * step, 1), high)
    return parts


def unrolled_columns(piece):
    block = lane_block(PIECE)
    rows = [None] * 16
    zero = jnp.zeros_like(piece)
    for j in range(OCT):
        turned = pltpu.roll(piece, PIECE * j, 1) if j else piece
        rows[7 - j] = jnp.where(block >= j, turned, zero).astype(BF16)
        rows[15 - j] = jnp.where(block < j, turned, zero).astype(BF16)
    return jnp.concatenate(rows, axis=0)


def shifted_filters(filters_ref, g_ref, padded_ref, stretches):
    groups = filters_ref.shape[0]
    width = padded_ref.shape[1]
    row = lax.broadcasted_iota(jnp.int32, (128, 128), 0)
    col = lax.broadcasted_iota(jnp.int32, (128, 128), 1)
    flip = (row + col == 127).astype(BF16)
    for n in range(stretches):
        chunk = filters_ref[:, 128 * (stretches - 1 - n) : 128 * (stretches - n)]
        padded_ref[:, 128 * n : 128 * (n + 1)] = jnp.dot(chunk, flip, preferred_element_type=F32)
    padded_ref[:, 128 * stretches :] = jnp.zeros((groups, width - 128 * stretches), F32)
    for g in range(groups):
        spread = jnp.broadcast_to(padded_ref[g : g + 1, :], (PIECE, width))
        turned = pltpu.roll(spread, width - 15, 1, stride=1, stride_axis=0).astype(BF16)
        for n in range(stretches + 2):
            g_ref[g, n] = turned[:, 128 * n : 128 * (n + 1)]


def conv_kernel(
    sources_ref, owner_ref, key_ref, value_ref, query_ref, window_ref, filters_ref,
    out_ref, g_ref, padded_ref, slot_ref,
):
    stretches = owner_ref.shape[0]
    slots = key_ref.shape[0] // STRETCH
    me = lax.axis_index("seq")
    last = stretches - 1
    count = jnp.int32(0)
    for k in range(stretches):
        slot_ref[count] = k
        count = count + jnp.where(owner_ref[k] == me, 1, 0)

    shifted_filters(filters_ref, g_ref, padded_ref, stretches)

    own_last = owner_ref[last] == me
    local = key_ref[(slots - 1) * STRETCH :, :].astype(F32) * value_ref[
        (slots - 1) * STRETCH :, :
    ].astype(F32)
    local = jnp.where(own_last, local.astype(BF16).astype(F32), 0.0)

    pieces = []
    for w in range(WIN):
        rows = local if w == WIN - 1 else window_ref[w].astype(F32)
        pieces.append(
            block_transpose([rows[PIECE * e : PIECE * (e + 1), :] for e in range(OCT)])
        )
    firsts = []
    for t in range(slots):
        target = slot_ref[t]
        firsts.append(
            [last - jnp.maximum(target - sources_ref[w], -1) for w in range(WIN)]
        )
    results = []
    for g in range(OCT):
        columns = jnp.concatenate([unrolled_columns(pieces[w][g]) for w in range(WIN)], axis=0)
        taps = jnp.concatenate(
            [
                jnp.concatenate(
                    [g_ref[g, firsts[t][w] + half] for w in range(WIN) for half in range(2)],
                    axis=1,
                )
                for t in range(slots)
            ],
            axis=0,
        )
        results.append(jnp.dot(taps, columns, preferred_element_type=F32))
    for t in range(slots):
        rows = block_transpose(
            [results[g][PIECE * t : PIECE * (t + 1), :] for g in range(OCT)]
        )
        for a in range(OCT):
            at = slice(STRETCH * t + PIECE * a, STRETCH * t + PIECE * (a + 1))
            out_ref[at, :] = (query_ref[at, :].astype(F32) * rows[a]).astype(BF16)


def conv(key_proj, value_proj, query_proj, window, filters, sources, owner):
    rows, channels = key_proj.shape
    groups, lags = filters.shape
    stretches = owner.shape[0]
    slots = rows // STRETCH
    wide = pl.BlockSpec((rows, 128), lambda o, *_: (0, o))
    return pl.pallas_call(
        conv_kernel,
        out_shape=jax.ShapeDtypeStruct((rows, channels), BF16),
        grid_spec=pltpu.PrefetchScalarGridSpec(
            num_scalar_prefetch=2,
            grid=(channels // 128,),
            in_specs=[
                wide,
                wide,
                wide,
                pl.BlockSpec((WIN - 1, STRETCH, 128), lambda o, *_: (0, 0, o)),
                pl.BlockSpec((OCT, lags), lambda o, *_: (o, 0)),
            ],
            out_specs=wide,
            scratch_shapes=[
                pltpu.VMEM((OCT, stretches + 2, PIECE, 128), BF16),
                pltpu.VMEM((OCT, lags + 256), F32),
                pltpu.SMEM((slots + 1,), jnp.int32),
            ],
        ),
        compiler_params=pltpu.CompilerParams(vmem_limit_bytes=48 * 2**20),
        cost_estimate=pl.CostEstimate(flops=2**30, bytes_accessed=6 * 2**20, transcendentals=0),
    )(sources, owner, key_proj, value_proj, query_proj, window, filters)


def shards(key_proj, value_proj, query_proj, filters, sources, owner):
    myself = lax.axis_index("seq")
    stretches = owner.shape[0]
    numbers = jnp.arange(stretches, dtype=jnp.int32)
    parts = []
    for w in range(WIN - 1):
        source = sources[w]
        hit = numbers == source
        source_owner = jnp.sum(jnp.where(hit, owner, 0))
        slot = jnp.sum(jnp.where((owner == source_owner) & (numbers < source), 1, 0))
        start = slot * STRETCH
        keys = lax.dynamic_slice_in_dim(key_proj, start, STRETCH, 0).astype(F32)
        values = lax.dynamic_slice_in_dim(value_proj, start, STRETCH, 0).astype(F32)
        gated = (keys * values).astype(BF16)
        parts.append(jnp.where(source_owner == myself, gated, jnp.zeros_like(gated)))
    window = lax.psum(jnp.stack(parts), "seq")
    lag_values = lax.all_gather(filters, "seq", axis=1, tiled=True)
    return conv(key_proj, value_proj, query_proj, window, lag_values, sources, owner)


def solution(mesh):
    return jax.shard_map(
        shards,
        mesh=mesh,
        in_specs=(
            P(("rep", "seq"), "ch"),
            P(("rep", "seq"), "ch"),
            P(("rep", "seq"), "ch"),
            P("ch", "seq"),
            P("rep"),
            P("rep"),
        ),
        out_specs=P(("rep", "seq"), "ch"),
        check_vma=False,
    )
```

```python
import functools

import jax
import jax.numpy as jnp
from jax import lax
from jax.experimental import pallas as pl
from jax.experimental.pallas import tpu as pltpu
from jax.sharding import PartitionSpec as P

GROUP_CH = 16
STRETCH = 128
WIN = 4
PIECE = 16
OCT = 8
F32 = jnp.float32
BF16 = jnp.bfloat16


def lane_block(rows):
    return lax.broadcasted_iota(jnp.int32, (rows, 128), 1) // PIECE


def block_transpose(parts):
    parts = list(parts)
    block = lane_block(parts[0].shape[0])
    for step in (1, 2, 4):
        keep = (block & step) == 0
        for p in range(OCT):
            if p & step:
                continue
            low, high = parts[p], parts[p + step]
            parts[p] = jnp.where(keep, low, pltpu.roll(high, PIECE * step, 1))
            parts[p + step] = jnp.where(keep, pltpu.roll(low, 128 - PIECE * step, 1), high)
    return parts


def unrolled_columns(piece):
    block = lane_block(PIECE)
    rows = [None] * 16
    zero = jnp.zeros_like(piece)
    for j in range(OCT):
        turned = pltpu.roll(piece, PIECE * j, 1) if j else piece
        rows[7 - j] = jnp.where(block >= j, turned, zero).astype(BF16)
        rows[15 - j] = jnp.where(block < j, turned, zero).astype(BF16)
    return jnp.concatenate(rows, axis=0)


def turn_filters(shards_ref, padded_ref):
    count, groups, span = shards_ref.shape
    width = padded_ref.shape[1]
    lags = count * span
    row = lax.broadcasted_iota(jnp.int32, (128, 128), 0)
    col = lax.broadcasted_iota(jnp.int32, (128, 128), 1)
    flip = (row + col == 127).astype(BF16)
    for n in range(lags // 128):
        at = lags - 128 * (n + 1)
        chunk = shards_ref[at // span, :, at % span : at % span + 128]
        padded_ref[:, 128 * n : 128 * (n + 1)] = jnp.dot(chunk, flip, preferred_element_type=F32)
    padded_ref[:, lags:] = jnp.zeros((groups, width - lags), F32)


def fused_kernel(
    size, sources_ref, owner_ref, key_ref, value_ref, query_ref, filters_ref,
    out_ref, right_ref, left_ref, from_left_ref, from_right_ref, taps_ref, padded_ref, g_ref,
    own_sem, tap_right_send, tap_left_send, tap_recv,
    right_send, right_recv, left_send, left_recv,
):
    stretches = owner_ref.shape[0]
    slots = key_ref.shape[0]
    octets = key_ref.shape[2] // 128
    width = padded_ref.shape[1]
    last = stretches - 1
    me = lax.axis_index("seq")
    has_left = me > 0
    has_right = me < size - 1

    def hop(src, dst, send, recv, step):
        return pltpu.make_async_remote_copy(
            src_ref=src, dst_ref=dst, send_sem=send, recv_sem=recv,
            device_id={"seq": me + step}, device_id_type=pl.DeviceIdType.MESH,
        )

    def tap_hop(shard, step):
        send = tap_right_send if step > 0 else tap_left_send
        return hop(
            taps_ref.at[shard], taps_ref.at[shard], send.at[shard], tap_recv.at[shard], step
        )

    def right_hop(o):
        return hop(right_ref.at[o], from_left_ref.at[o], right_send.at[o], right_recv.at[o], 1)

    def left_hop(o):
        return hop(left_ref.at[o], from_right_ref.at[o], left_send.at[o], left_recv.at[o], -1)

    own_taps = pltpu.make_async_copy(filters_ref, taps_ref.at[me], own_sem)
    own_taps.start()
    barrier = pltpu.get_barrier_semaphore()

    @pl.when(has_left)
    def _():
        pl.semaphore_signal(
            barrier, inc=1, device_id={"seq": me - 1}, device_id_type=pl.DeviceIdType.MESH
        )

    @pl.when(has_right)
    def _():
        pl.semaphore_signal(
            barrier, inc=1, device_id={"seq": me + 1}, device_id_type=pl.DeviceIdType.MESH
        )

    source = [sources_ref[w] for w in range(WIN)]
    holders = [owner_ref[k] for k in range(stretches)]
    source_owner = [
        sum(jnp.where(source[w] == k, holders[k], 0) for k in range(stretches)) for w in range(WIN)
    ]
    source_slot = [jnp.int32(0)] * WIN
    slot_stretch = [jnp.int32(0)] * slots
    count = jnp.int32(0)
    for k in range(stretches):
        holder = holders[k]
        for w in range(WIN - 1):
            source_slot[w] += jnp.where((holder == source_owner[w]) & (k < source[w]), 1, 0)
        here = holder == me
        for t in range(slots):
            slot_stretch[t] += jnp.where(here & (count == t), k, 0)
        count += jnp.where(here, 1, 0)
    owners = [jnp.full((STRETCH, 128), source_owner[w], jnp.int32) for w in range(WIN)]

    def choose(mask, yes, no):
        return jnp.where(mask, yes.astype(F32), no.astype(F32))

    first = [
        [last - jnp.maximum(slot_stretch[t] - source[w], -1) for w in range(WIN)]
        for t in range(slots)
    ]

    def gated(slot, o):
        at = (slot, slice(None), pl.ds(pl.multiple_of(o * 128, 128), 128))
        return (key_ref[at].astype(F32) * value_ref[at].astype(F32)).astype(BF16)

    own_taps.wait()

    pl.semaphore_wait(barrier, has_left.astype(jnp.int32) + has_right.astype(jnp.int32))

    @pl.when(has_right)
    def _():
        tap_hop(me, 1).start()

    @pl.when(has_left)
    def _():
        tap_hop(me, -1).start()

    @pl.loop(0, octets)
    def _(o):
        for w in range(WIN - 1):
            piece = gated(source_slot[w], o)
            right_ref[o, w] = piece
            left_ref[o, w] = piece

        @pl.when(jnp.logical_not(has_left))
        def _():
            right_hop(o).start()

        @pl.when(jnp.logical_not(has_right))
        def _():
            left_hop(o).start()

    for d in range(1, size):
        @pl.when(me >= d)
        def _():
            tap_hop(me - d, -1).wait_recv()

            @pl.when(has_right)
            def _():
                tap_hop(me - d, 1).start()

        @pl.when(me + d < size)
        def _():
            tap_hop(me + d, 1).wait_recv()

            @pl.when(has_left)
            def _():
                tap_hop(me + d, -1).start()

    turn_filters(taps_ref, padded_ref)

    @pl.loop(0, octets)
    def _(o):
        spans = padded_ref[pl.ds(pl.multiple_of(o * OCT, OCT), OCT), :]
        for g in range(OCT):
            spread = jnp.broadcast_to(spans[g : g + 1, :], (PIECE, width))
            turned = pltpu.roll(spread, width - 15, 1, stride=1, stride_axis=0).astype(BF16)
            for n in range(stretches + 2):
                g_ref[g, n] = turned[:, 128 * n : 128 * (n + 1)]

        @pl.when(has_left)
        def _():
            right_hop(o).wait_recv()
            for w in range(WIN - 1):
                right_ref[o, w] = choose(
                    owners[w] == me, right_ref[o, w], from_left_ref[o, w]
                ).astype(BF16)

            @pl.when(has_right)
            def _():
                right_hop(o).start()

        @pl.when(has_right)
        def _():
            left_hop(o).wait_recv()
            for w in range(WIN - 1):
                left_ref[o, w] = choose(
                    owners[w] == me, left_ref[o, w], from_right_ref[o, w]
                ).astype(BF16)

            @pl.when(has_left)
            def _():
                left_hop(o).start()

        pieces = []
        for w in range(WIN):
            if w == WIN - 1:
                rows = gated(slots - 1, o)
                rows = choose(owners[w] == me, rows, jnp.zeros_like(rows))
            else:
                rows = choose(owners[w] <= me, right_ref[o, w], left_ref[o, w])
            pieces.append(
                block_transpose([rows[PIECE * e : PIECE * (e + 1), :] for e in range(OCT)])
            )
        results = []
        for g in range(OCT):
            columns = jnp.concatenate(
                [unrolled_columns(pieces[w][g]) for w in range(WIN)], axis=0
            )
            taps = jnp.concatenate(
                [
                    jnp.concatenate(
                        [g_ref[g, first[t][w] + half] for w in range(WIN) for half in range(2)],
                        axis=1,
                    )
                    for t in range(slots)
                ],
                axis=0,
            )
            results.append(jnp.dot(taps, columns, preferred_element_type=F32))
        lanes = pl.ds(pl.multiple_of(o * 128, 128), 128)
        for t in range(slots):
            rows = block_transpose(
                [results[g][PIECE * t : PIECE * (t + 1), :] for g in range(OCT)]
            )
            for a in range(OCT):
                at = (slice(STRETCH * t + PIECE * a, STRETCH * t + PIECE * (a + 1)), lanes)
                out_ref[at] = (query_ref[at].astype(F32) * rows[a]).astype(BF16)

    for shard in range(size):
        @pl.when(has_right & (me >= shard))
        def _():
            tap_hop(shard, 1).wait_send()

        @pl.when(has_left & (me <= shard))
        def _():
            tap_hop(shard, -1).wait_send()

    @pl.loop(0, octets)
    def _(o):
        @pl.when(has_right)
        def _():
            right_hop(o).wait_send()

        @pl.when(has_left)
        def _():
            left_hop(o).wait_send()


def shards(size, key_proj, value_proj, query_proj, filters, sources, owner):
    rows, channels = key_proj.shape
    groups, span = filters.shape
    stretches = owner.shape[0]
    octets = channels // 128
    lags = size * span
    by_slot = (rows // STRETCH, STRETCH, channels)
    key_proj, value_proj = key_proj.reshape(by_slot), value_proj.reshape(by_slot)
    vmem = pl.BlockSpec(memory_space=pltpu.VMEM)
    smem = pl.BlockSpec(memory_space=pltpu.SMEM)
    chunk = pltpu.VMEM((octets, WIN - 1, STRETCH, 128), BF16)
    dma = pltpu.SemaphoreType.DMA
    return pl.pallas_call(
        functools.partial(fused_kernel, size),
        out_shape=jax.ShapeDtypeStruct((rows, channels), BF16),
        in_specs=[smem, smem, vmem, vmem, vmem, vmem],
        out_specs=vmem,
        scratch_shapes=[
            chunk, chunk, chunk, chunk,
            pltpu.VMEM((size, groups, span), BF16),
            pltpu.VMEM((groups, lags + 256), F32),
            pltpu.VMEM((OCT, stretches + 2, PIECE, 128), BF16),
            dma, dma((size,)), dma((size,)), dma((size,)),
            dma((octets,)), dma((octets,)), dma((octets,)), dma((octets,)),
        ],
        compiler_params=pltpu.CompilerParams(
            vmem_limit_bytes=48 * 2**20, collective_id=0, has_side_effects=True
        ),
    )(sources, owner, key_proj, value_proj, query_proj, filters)


def solution(mesh):
    return jax.shard_map(
        functools.partial(shards, mesh.shape["seq"]),
        mesh=mesh,
        in_specs=(
            P(("rep", "seq"), "ch"),
            P(("rep", "seq"), "ch"),
            P(("rep", "seq"), "ch"),
            P("ch", "seq"),
            P("rep"),
            P("rep"),
        ),
        out_specs=P(("rep", "seq"), "ch"),
        check_vma=False,
    )
```

```python
import functools

import jax
import jax.numpy as jnp
from jax import lax
from jax.experimental import pallas as pl
from jax.experimental.pallas import tpu as pltpu
from jax.sharding import PartitionSpec as P

GROUP_CH = 16
STRETCH = 128
WIN = 4
PIECE = 16
OCT = 8
AHEAD = 1
F32 = jnp.float32
BF16 = jnp.bfloat16


def lane_block(rows):
    return lax.broadcasted_iota(jnp.int32, (rows, 128), 1) // PIECE


def block_transpose(parts):
    parts = list(parts)
    block = lane_block(parts[0].shape[0])
    for step in (1, 2, 4):
        keep = (block & step) == 0
        for p in range(OCT):
            if p & step:
                continue
            low, high = parts[p], parts[p + step]
            parts[p] = jnp.where(keep, low, pltpu.roll(high, PIECE * step, 1))
            parts[p + step] = jnp.where(keep, pltpu.roll(low, 128 - PIECE * step, 1), high)
    return parts


def unrolled_columns(piece):
    block = lane_block(PIECE)
    rows = [None] * 16
    zero = jnp.zeros_like(piece)
    for j in range(OCT):
        turned = pltpu.roll(piece, PIECE * j, 1) if j else piece
        rows[7 - j] = jnp.where(block >= j, turned, zero).astype(BF16)
        rows[15 - j] = jnp.where(block < j, turned, zero).astype(BF16)
    return jnp.concatenate(rows, axis=0)


def turn_filters(shards_ref, padded_ref):
    count, groups, span = shards_ref.shape
    width = padded_ref.shape[1]
    lags = count * span
    row = lax.broadcasted_iota(jnp.int32, (128, 128), 0)
    col = lax.broadcasted_iota(jnp.int32, (128, 128), 1)
    flip = (row + col == 127).astype(BF16)
    for n in range(lags // 128):
        at = lags - 128 * (n + 1)
        chunk = shards_ref[at // span, :, at % span : at % span + 128]
        padded_ref[:, 128 * n : 128 * (n + 1)] = jnp.dot(chunk, flip, preferred_element_type=F32)
    padded_ref[:, lags:] = jnp.zeros((groups, width - lags), F32)


def fused_kernel(
    size, sources_ref, owner_ref, key_hbm, value_hbm, query_hbm, filters_ref,
    out_ref, key_ref, value_ref, query_ref, right_ref, left_ref, from_left_ref, from_right_ref, taps_ref, padded_ref, g_ref,
    own_sem, load_sem, tap_right_send, tap_left_send, tap_recv,
    right_send, right_recv, left_send, left_recv,
):
    stretches = owner_ref.shape[0]
    slots = key_ref.shape[0]
    octets = key_ref.shape[2] // 128
    width = padded_ref.shape[1]
    last = stretches - 1
    me = lax.axis_index("seq")
    has_left = me > 0
    has_right = me < size - 1

    def hop(src, dst, send, recv, step):
        return pltpu.make_async_remote_copy(
            src_ref=src, dst_ref=dst, send_sem=send, recv_sem=recv,
            device_id={"seq": me + step}, device_id_type=pl.DeviceIdType.MESH,
        )

    def tap_hop(shard, step):
        send = tap_right_send if step > 0 else tap_left_send
        return hop(
            taps_ref.at[shard], taps_ref.at[shard], send.at[shard], tap_recv.at[shard], step
        )

    def right_hop(o):
        return hop(right_ref.at[o], from_left_ref.at[o], right_send.at[o], right_recv.at[o], 1)

    def left_hop(o):
        return hop(left_ref.at[o], from_right_ref.at[o], left_send.at[o], left_recv.at[o], -1)

    own_taps = pltpu.make_async_copy(filters_ref, taps_ref.at[me], own_sem)
    own_taps.start()
    loads = [
        pltpu.make_async_copy(src, dst, load_sem.at[i])
        for i, (src, dst) in enumerate(
            ((key_hbm, key_ref), (value_hbm, value_ref), (query_hbm, query_ref))
        )
    ]
    for load in loads:
        load.start()
    barrier = pltpu.get_barrier_semaphore()

    @pl.when(has_left)
    def _():
        pl.semaphore_signal(
            barrier, inc=1, device_id={"seq": me - 1}, device_id_type=pl.DeviceIdType.MESH
        )

    @pl.when(has_right)
    def _():
        pl.semaphore_signal(
            barrier, inc=1, device_id={"seq": me + 1}, device_id_type=pl.DeviceIdType.MESH
        )

    source = [sources_ref[w] for w in range(WIN)]
    holders = [owner_ref[k] for k in range(stretches)]
    source_owner = [
        sum(jnp.where(source[w] == k, holders[k], 0) for k in range(stretches)) for w in range(WIN)
    ]
    source_slot = [jnp.int32(0)] * WIN
    slot_stretch = [jnp.int32(0)] * slots
    count = jnp.int32(0)
    for k in range(stretches):
        holder = holders[k]
        for w in range(WIN - 1):
            source_slot[w] += jnp.where((holder == source_owner[w]) & (k < source[w]), 1, 0)
        here = holder == me
        for t in range(slots):
            slot_stretch[t] += jnp.where(here & (count == t), k, 0)
        count += jnp.where(here, 1, 0)
    owners = [jnp.full((STRETCH, 128), source_owner[w], jnp.int32) for w in range(WIN)]

    def choose(mask, yes, no):
        return jnp.where(mask, yes.astype(F32), no.astype(F32))

    first = [
        [last - jnp.maximum(slot_stretch[t] - source[w], -1) for w in range(WIN)]
        for t in range(slots)
    ]

    def gated(slot, o):
        at = (slot, slice(None), pl.ds(pl.multiple_of(o * 128, 128), 128))
        return (key_ref[at].astype(F32) * value_ref[at].astype(F32)).astype(BF16)

    own_taps.wait()

    pl.semaphore_wait(barrier, has_left.astype(jnp.int32) + has_right.astype(jnp.int32))

    @pl.when(has_right)
    def _():
        tap_hop(me, 1).start()

    @pl.when(has_left)
    def _():
        tap_hop(me, -1).start()

    for load in loads:
        load.wait()

    @pl.loop(0, octets)
    def _(o):
        for w in range(WIN - 1):
            piece = gated(source_slot[w], o)
            right_ref[o, w] = piece
            left_ref[o, w] = piece

    right_lag = me
    left_lag = size - 1 - me
    lag = jnp.maximum(right_lag, left_lag)

    @pl.loop(0, octets + size - 1)
    def _(s):
        @pl.when((s >= 1) & (me >= s))
        def _():
            tap_hop(me - s, -1).wait_recv()

            @pl.when(has_right)
            def _():
                tap_hop(me - s, 1).start()

        @pl.when((s >= 1) & (me + s < size))
        def _():
            tap_hop(me + s, 1).wait_recv()

            @pl.when(has_left)
            def _():
                tap_hop(me + s, -1).start()

        @pl.when((s >= right_lag) & (s < right_lag + octets))
        def _():
            o = s - right_lag

            @pl.when(has_left)
            def _():
                right_hop(o).wait_recv()
                for w in range(WIN - 1):
                    right_ref[o, w] = choose(
                        owners[w] == me, right_ref[o, w], from_left_ref[o, w]
                    ).astype(BF16)

            @pl.when(has_right)
            def _():
                @pl.when(o >= AHEAD)
                def _():
                    right_hop(o - AHEAD).wait_send()

                right_hop(o).start()

        @pl.when((s >= left_lag) & (s < left_lag + octets))
        def _():
            o = s - left_lag

            @pl.when(has_right)
            def _():
                left_hop(o).wait_recv()
                for w in range(WIN - 1):
                    left_ref[o, w] = choose(
                        owners[w] == me, left_ref[o, w], from_right_ref[o, w]
                    ).astype(BF16)

            @pl.when(has_left)
            def _():
                @pl.when(o >= AHEAD)
                def _():
                    left_hop(o - AHEAD).wait_send()

                left_hop(o).start()

        @pl.when(s == lag)
        def _():
            turn_filters(taps_ref, padded_ref)

        @pl.when((s >= lag) & (s < lag + octets))
        def _():
            o = s - lag
            spans = padded_ref[pl.ds(pl.multiple_of(o * OCT, OCT), OCT), :]
            for g in range(OCT):
                spread = jnp.broadcast_to(spans[g : g + 1, :], (PIECE, width))
                turned = pltpu.roll(spread, width - 15, 1, stride=1, stride_axis=0).astype(BF16)
                for n in range(stretches + 2):
                    g_ref[g, n] = turned[:, 128 * n : 128 * (n + 1)]

            pieces = []
            for w in range(WIN):
                if w == WIN - 1:
                    rows = gated(slots - 1, o)
                    rows = choose(owners[w] == me, rows, jnp.zeros_like(rows))
                else:
                    rows = choose(owners[w] <= me, right_ref[o, w], left_ref[o, w])
                pieces.append(
                    block_transpose([rows[PIECE * e : PIECE * (e + 1), :] for e in range(OCT)])
                )
            results = []
            for g in range(OCT):
                columns = jnp.concatenate(
                    [unrolled_columns(pieces[w][g]) for w in range(WIN)], axis=0
                )
                taps = jnp.concatenate(
                    [
                        jnp.concatenate(
                            [g_ref[g, first[t][w] + half] for w in range(WIN) for half in range(2)],
                            axis=1,
                        )
                        for t in range(slots)
                    ],
                    axis=0,
                )
                results.append(jnp.dot(taps, columns, preferred_element_type=F32))
            lanes = pl.ds(pl.multiple_of(o * 128, 128), 128)
            for t in range(slots):
                rows = block_transpose(
                    [results[g][PIECE * t : PIECE * (t + 1), :] for g in range(OCT)]
                )
                for a in range(OCT):
                    at = (slice(STRETCH * t + PIECE * a, STRETCH * t + PIECE * (a + 1)), lanes)
                    out_ref[at] = (query_ref[at].astype(F32) * rows[a]).astype(BF16)

    for shard in range(size):
        @pl.when(has_right & (me >= shard))
        def _():
            tap_hop(shard, 1).wait_send()

        @pl.when(has_left & (me <= shard))
        def _():
            tap_hop(shard, -1).wait_send()

    @pl.loop(max(octets - AHEAD, 0), octets)
    def _(o):
        @pl.when(has_right)
        def _():
            right_hop(o).wait_send()

        @pl.when(has_left)
        def _():
            left_hop(o).wait_send()


def shards(size, key_proj, value_proj, query_proj, filters, sources, owner):
    rows, channels = key_proj.shape
    groups, span = filters.shape
    stretches = owner.shape[0]
    octets = channels // 128
    lags = size * span
    by_slot = (rows // STRETCH, STRETCH, channels)
    key_proj, value_proj = key_proj.reshape(by_slot), value_proj.reshape(by_slot)
    vmem = pl.BlockSpec(memory_space=pltpu.VMEM)
    hbm = pl.BlockSpec(memory_space=pl.ANY)
    smem = pl.BlockSpec(memory_space=pltpu.SMEM)
    chunk = pltpu.VMEM((octets, WIN - 1, STRETCH, 128), BF16)
    dma = pltpu.SemaphoreType.DMA
    return pl.pallas_call(
        functools.partial(fused_kernel, size),
        out_shape=jax.ShapeDtypeStruct((rows, channels), BF16),
        in_specs=[smem, smem, hbm, hbm, hbm, hbm],
        out_specs=vmem,
        scratch_shapes=[
            pltpu.VMEM(by_slot, BF16), pltpu.VMEM(by_slot, BF16), pltpu.VMEM((rows, channels), BF16),
            chunk, chunk, chunk, chunk,
            pltpu.VMEM((size, groups, span), BF16),
            pltpu.VMEM((groups, lags + 256), F32),
            pltpu.VMEM((OCT, stretches + 2, PIECE, 128), BF16),
            dma, dma((3,)), dma((size,)), dma((size,)), dma((size,)),
            dma((octets,)), dma((octets,)), dma((octets,)), dma((octets,)),
        ],
        compiler_params=pltpu.CompilerParams(
            vmem_limit_bytes=60 * 2**20, collective_id=0, has_side_effects=True
        ),
    )(sources, owner, key_proj, value_proj, query_proj, filters)


def solution(mesh):
    return jax.shard_map(
        functools.partial(shards, mesh.shape["seq"]),
        mesh=mesh,
        in_specs=(
            P(("rep", "seq"), "ch"),
            P(("rep", "seq"), "ch"),
            P(("rep", "seq"), "ch"),
            P("ch", "seq"),
            P("rep"),
            P("rep"),
        ),
        out_specs=P(("rep", "seq"), "ch"),
        check_vma=False,
    )
```

```python
import functools

import jax
import jax.numpy as jnp
from jax import lax
from jax.experimental import pallas as pl
from jax.experimental.pallas import tpu as pltpu
from jax.sharding import PartitionSpec as P

GROUP_CH = 16
STRETCH = 128
WIN = 4
PIECE = 16
OCT = 8
AHEAD = 8
HOP = 6
SENT = WIN - 1
F32 = jnp.float32
BF16 = jnp.bfloat16


def lane_block(rows):
    return lax.broadcasted_iota(jnp.int32, (rows, 128), 1) // PIECE


def block_transpose(parts):
    parts = list(parts)
    block = lane_block(parts[0].shape[0])
    for step in (1, 2, 4):
        keep = (block & step) == 0
        for p in range(OCT):
            if p & step:
                continue
            low, high = parts[p], parts[p + step]
            parts[p] = jnp.where(keep, low, pltpu.roll(high, PIECE * step, 1))
            parts[p + step] = jnp.where(keep, pltpu.roll(low, 128 - PIECE * step, 1), high)
    return parts


def unrolled_columns(piece):
    block = lane_block(PIECE)
    rows = [None] * 16
    zero = jnp.zeros_like(piece)
    for j in range(OCT):
        turned = pltpu.roll(piece, PIECE * j, 1) if j else piece
        rows[7 - j] = jnp.where(block >= j, turned, zero).astype(BF16)
        rows[15 - j] = jnp.where(block < j, turned, zero).astype(BF16)
    return jnp.concatenate(rows, axis=0)


def turn_filters(shards_ref, padded_ref):
    count, groups, span = shards_ref.shape
    width = padded_ref.shape[1]
    lags = count * span
    row = lax.broadcasted_iota(jnp.int32, (128, 128), 0)
    col = lax.broadcasted_iota(jnp.int32, (128, 128), 1)
    flip = (row + col == 127).astype(BF16)
    for n in range(lags // 128):
        at = lags - 128 * (n + 1)
        chunk = shards_ref[at // span, :, at % span : at % span + 128]
        padded_ref[:, 128 * n : 128 * (n + 1)] = jnp.dot(chunk, flip, preferred_element_type=F32)
    padded_ref[:, lags:] = jnp.zeros((groups, width - lags), F32)


def fused_kernel(
    size, sources_ref, owner_ref, key_hbm, value_hbm, query_hbm, filters_ref,
    out_ref, key_ref, value_ref, query_ref, right_ref, left_ref, from_left_ref, from_right_ref, taps_ref, padded_ref, g_ref,
    own_sem, load_sem, tap_right_send, tap_left_send, tap_recv,
    right_send, right_recv, left_send, left_recv,
):
    stretches = owner_ref.shape[0]
    slots = key_ref.shape[0]
    octets = key_ref.shape[2] // 128
    width = padded_ref.shape[1]
    last = stretches - 1
    me = lax.axis_index("seq")
    has_left = me > 0
    has_right = me < size - 1

    def hop(src, dst, send, recv, step):
        return pltpu.make_async_remote_copy(
            src_ref=src, dst_ref=dst, send_sem=send, recv_sem=recv,
            device_id={"seq": me + step}, device_id_type=pl.DeviceIdType.MESH,
        )

    def tap_hop(shard, step):
        send = tap_right_send if step > 0 else tap_left_send
        return hop(
            taps_ref.at[shard], taps_ref.at[shard], send.at[shard], tap_recv.at[shard], step
        )

    def right_hop(o):
        return hop(right_ref.at[o], from_left_ref.at[o], right_send.at[o], right_recv.at[o], 1)

    def left_hop(o):
        return hop(left_ref.at[o], from_right_ref.at[o], left_send.at[o], left_recv.at[o], -1)

    own_taps = pltpu.make_async_copy(filters_ref, taps_ref.at[me], own_sem)
    own_taps.start()
    loads = [
        pltpu.make_async_copy(src, dst, load_sem.at[i])
        for i, (src, dst) in enumerate(
            ((key_hbm, key_ref), (value_hbm, value_ref), (query_hbm, query_ref))
        )
    ]
    for load in loads:
        load.start()
    barrier = pltpu.get_barrier_semaphore()

    @pl.when(has_left)
    def _():
        pl.semaphore_signal(
            barrier, inc=1, device_id={"seq": me - 1}, device_id_type=pl.DeviceIdType.MESH
        )

    @pl.when(has_right)
    def _():
        pl.semaphore_signal(
            barrier, inc=1, device_id={"seq": me + 1}, device_id_type=pl.DeviceIdType.MESH
        )

    source = [sources_ref[w] for w in range(WIN)]
    holders = [owner_ref[k] for k in range(stretches)]
    source_owner = [
        sum(jnp.where(source[w] == k, holders[k], 0) for k in range(stretches)) for w in range(WIN)
    ]
    source_slot = [jnp.int32(0)] * WIN
    slot_stretch = [jnp.int32(0)] * slots
    count = jnp.int32(0)
    for k in range(stretches):
        holder = holders[k]
        for w in range(WIN - 1):
            source_slot[w] += jnp.where((holder == source_owner[w]) & (k < source[w]), 1, 0)
        here = holder == me
        for t in range(slots):
            slot_stretch[t] += jnp.where(here & (count == t), k, 0)
        count += jnp.where(here, 1, 0)
    chunks = octets * SENT

    def is_mine(c):
        w = c % SENT
        holder = sum(jnp.where(w == k, source_owner[k], 0) for k in range(SENT))
        return jnp.full((STRETCH, 128), holder, jnp.int32) == me

    owners = [jnp.full((STRETCH, 128), source_owner[w], jnp.int32) for w in range(WIN)]

    def choose(mask, yes, no):
        return jnp.where(mask, yes.astype(F32), no.astype(F32))

    first = [
        [last - jnp.maximum(slot_stretch[t] - source[w], -1) for w in range(WIN)]
        for t in range(slots)
    ]

    def gated(slot, o):
        at = (slot, slice(None), pl.ds(pl.multiple_of(o * 128, 128), 128))
        return (key_ref[at].astype(F32) * value_ref[at].astype(F32)).astype(BF16)

    own_taps.wait()

    pl.semaphore_wait(barrier, has_left.astype(jnp.int32) + has_right.astype(jnp.int32))

    @pl.when(has_right)
    def _():
        tap_hop(me, 1).start()

    @pl.when(has_left)
    def _():
        tap_hop(me, -1).start()

    loads[0].wait()
    loads[1].wait()

    @pl.loop(0, octets)
    def _(o):
        for w in range(WIN - 1):
            piece = gated(source_slot[w], o)
            right_ref[o * SENT + w] = piece
            left_ref[o * SENT + w] = piece

    right_lag = HOP * me
    left_lag = HOP * (size - 1 - me)
    lag = jnp.maximum(right_lag, left_lag)

    @pl.loop(0, chunks + HOP * (size - 1))
    def _(s):
        far = s // HOP
        turn = (s % HOP == 0) & (far >= 1)

        @pl.when(turn & (me >= far))
        def _():
            tap_hop(me - far, -1).wait_recv()

            @pl.when(has_right)
            def _():
                tap_hop(me - far, 1).start()

        @pl.when(turn & (me + far < size))
        def _():
            tap_hop(me + far, 1).wait_recv()

            @pl.when(has_left)
            def _():
                tap_hop(me + far, -1).start()

        @pl.when((s >= right_lag) & (s < right_lag + chunks))
        def _():
            o = s - right_lag

            @pl.when(has_left)
            def _():
                right_hop(o).wait_recv()
                right_ref[o] = choose(is_mine(o), right_ref[o], from_left_ref[o]).astype(BF16)

            @pl.when(has_right)
            def _():
                @pl.when(o >= AHEAD)
                def _():
                    right_hop(o - AHEAD).wait_send()

                right_hop(o).start()

        @pl.when((s >= left_lag) & (s < left_lag + chunks))
        def _():
            o = s - left_lag

            @pl.when(has_right)
            def _():
                left_hop(o).wait_recv()
                left_ref[o] = choose(is_mine(o), left_ref[o], from_right_ref[o]).astype(BF16)

            @pl.when(has_left)
            def _():
                @pl.when(o >= AHEAD)
                def _():
                    left_hop(o - AHEAD).wait_send()

                left_hop(o).start()

        @pl.when(s == lag)
        def _():
            turn_filters(taps_ref, padded_ref)
            loads[2].wait()

        @pl.when((s >= lag) & (s < lag + chunks) & ((s - lag) % SENT == SENT - 1))
        def _():
            o = (s - lag) // SENT
            spans = padded_ref[pl.ds(pl.multiple_of(o * OCT, OCT), OCT), :]
            for g in range(OCT):
                spread = jnp.broadcast_to(spans[g : g + 1, :], (PIECE, width))
                turned = pltpu.roll(spread, width - 15, 1, stride=1, stride_axis=0).astype(BF16)
                for n in range(stretches + 2):
                    g_ref[g, n] = turned[:, 128 * n : 128 * (n + 1)]

            pieces = []
            for w in range(WIN):
                if w == WIN - 1:
                    rows = gated(slots - 1, o)
                    rows = choose(owners[w] == me, rows, jnp.zeros_like(rows))
                else:
                    rows = choose(owners[w] <= me, right_ref[o * SENT + w], left_ref[o * SENT + w])
                pieces.append(
                    block_transpose([rows[PIECE * e : PIECE * (e + 1), :] for e in range(OCT)])
                )
            results = []
            for g in range(OCT):
                columns = jnp.concatenate(
                    [unrolled_columns(pieces[w][g]) for w in range(WIN)], axis=0
                )
                taps = jnp.concatenate(
                    [
                        jnp.concatenate(
                            [g_ref[g, first[t][w] + half] for w in range(WIN) for half in range(2)],
                            axis=1,
                        )
                        for t in range(slots)
                    ],
                    axis=0,
                )
                results.append(jnp.dot(taps, columns, preferred_element_type=F32))
            lanes = pl.ds(pl.multiple_of(o * 128, 128), 128)
            for t in range(slots):
                rows = block_transpose(
                    [results[g][PIECE * t : PIECE * (t + 1), :] for g in range(OCT)]
                )
                for a in range(OCT):
                    at = (slice(STRETCH * t + PIECE * a, STRETCH * t + PIECE * (a + 1)), lanes)
                    out_ref[at] = (query_ref[at].astype(F32) * rows[a]).astype(BF16)

    for shard in range(size):
        @pl.when(has_right & (me >= shard))
        def _():
            tap_hop(shard, 1).wait_send()

        @pl.when(has_left & (me <= shard))
        def _():
            tap_hop(shard, -1).wait_send()

    @pl.loop(max(chunks - AHEAD, 0), chunks)
    def _(o):
        @pl.when(has_right)
        def _():
            right_hop(o).wait_send()

        @pl.when(has_left)
        def _():
            left_hop(o).wait_send()


def shards(size, key_proj, value_proj, query_proj, filters, sources, owner):
    rows, channels = key_proj.shape
    groups, span = filters.shape
    stretches = owner.shape[0]
    octets = channels // 128
    lags = size * span
    chunks = octets * SENT
    by_slot = (rows // STRETCH, STRETCH, channels)
    key_proj, value_proj = key_proj.reshape(by_slot), value_proj.reshape(by_slot)
    vmem = pl.BlockSpec(memory_space=pltpu.VMEM)
    hbm = pl.BlockSpec(memory_space=pl.ANY)
    smem = pl.BlockSpec(memory_space=pltpu.SMEM)
    chunk = pltpu.VMEM((chunks, STRETCH, 128), BF16)
    dma = pltpu.SemaphoreType.DMA
    return pl.pallas_call(
        functools.partial(fused_kernel, size),
        out_shape=jax.ShapeDtypeStruct((rows, channels), BF16),
        in_specs=[smem, smem, hbm, hbm, hbm, hbm],
        out_specs=vmem,
        scratch_shapes=[
            pltpu.VMEM(by_slot, BF16), pltpu.VMEM(by_slot, BF16), pltpu.VMEM((rows, channels), BF16),
            chunk, chunk, chunk, chunk,
            pltpu.VMEM((size, groups, span), BF16),
            pltpu.VMEM((groups, lags + 256), F32),
            pltpu.VMEM((OCT, stretches + 2, PIECE, 128), BF16),
            dma, dma((3,)), dma((size,)), dma((size,)), dma((size,)),
            dma((chunks,)), dma((chunks,)), dma((chunks,)), dma((chunks,)),
        ],
        compiler_params=pltpu.CompilerParams(
            vmem_limit_bytes=40 * 2**20, collective_id=0, has_side_effects=True
        ),
    )(sources, owner, key_proj, value_proj, query_proj, filters)


def solution(mesh):
    return jax.shard_map(
        functools.partial(shards, mesh.shape["seq"]),
        mesh=mesh,
        in_specs=(
            P(("rep", "seq"), "ch"),
            P(("rep", "seq"), "ch"),
            P(("rep", "seq"), "ch"),
            P("ch", "seq"),
            P("rep"),
            P("rep"),
        ),
        out_specs=P(("rep", "seq"), "ch"),
        check_vma=False,
    )
```

```python
import functools

import jax
import jax.numpy as jnp
from jax import lax
from jax.experimental import pallas as pl
from jax.experimental.pallas import tpu as pltpu
from jax.sharding import PartitionSpec as P

GROUP_CH = 16
STRETCH = 128
WIN = 4
PIECE = 16
OCT = 8
AHEAD = 8
HOP = 6
SENT = WIN - 1
F32 = jnp.float32
BF16 = jnp.bfloat16


def lane_block(rows):
    return lax.broadcasted_iota(jnp.int32, (rows, 128), 1) // PIECE


def block_transpose(parts):
    parts = list(parts)
    block = lane_block(parts[0].shape[0])
    for step in (1, 2, 4):
        keep = (block & step) == 0
        for p in range(OCT):
            if p & step:
                continue
            low, high = parts[p], parts[p + step]
            parts[p] = jnp.where(keep, low, pltpu.roll(high, PIECE * step, 1))
            parts[p + step] = jnp.where(keep, pltpu.roll(low, 128 - PIECE * step, 1), high)
    return parts


def unrolled_columns(piece):
    block = lane_block(PIECE)
    rows = [None] * 16
    for j in range(OCT):
        turned = pltpu.roll(piece, PIECE * j, 1) if j else piece
        turned = turned.astype(BF16)
        rows[7 - j] = turned * jnp.where(block >= j, 1.0, 0.0).astype(BF16)
        rows[15 - j] = turned * jnp.where(block < j, 1.0, 0.0).astype(BF16)
    return jnp.concatenate(rows, axis=0)


def turn_filters(shards_ref, padded_ref):
    count, groups, span = shards_ref.shape
    width = padded_ref.shape[1]
    lags = count * span
    row = lax.broadcasted_iota(jnp.int32, (128, 128), 0)
    col = lax.broadcasted_iota(jnp.int32, (128, 128), 1)
    flip = (row + col == 127).astype(BF16)
    for n in range(lags // 128):
        at = lags - 128 * (n + 1)
        chunk = shards_ref[at // span, :, at % span : at % span + 128]
        padded_ref[:, 128 * n : 128 * (n + 1)] = jnp.dot(chunk, flip, preferred_element_type=F32)
    padded_ref[:, lags:] = jnp.zeros((groups, width - lags), F32)


def fused_kernel(
    size, sources_ref, owner_ref, key_hbm, value_hbm, query_hbm, filters_ref,
    out_ref, key_ref, value_ref, query_ref, right_ref, left_ref, from_left_ref, from_right_ref, taps_ref, padded_ref, g_ref,
    own_sem, load_sem, tap_right_send, tap_left_send, tap_recv,
    right_send, right_recv, left_send, left_recv,
):
    stretches = owner_ref.shape[0]
    slots = key_ref.shape[0]
    octets = key_ref.shape[2] // 128
    width = padded_ref.shape[1]
    last = stretches - 1
    me = lax.axis_index("seq")
    has_left = me > 0
    has_right = me < size - 1

    def hop(src, dst, send, recv, step):
        return pltpu.make_async_remote_copy(
            src_ref=src, dst_ref=dst, send_sem=send, recv_sem=recv,
            device_id={"seq": me + step}, device_id_type=pl.DeviceIdType.MESH,
        )

    def tap_hop(shard, step):
        send = tap_right_send if step > 0 else tap_left_send
        return hop(
            taps_ref.at[shard], taps_ref.at[shard], send.at[shard], tap_recv.at[shard], step
        )

    def right_hop(o):
        return hop(right_ref.at[o], from_left_ref.at[o], right_send.at[o], right_recv.at[o], 1)

    def left_hop(o):
        return hop(left_ref.at[o], from_right_ref.at[o], left_send.at[o], left_recv.at[o], -1)

    own_taps = pltpu.make_async_copy(filters_ref, taps_ref.at[me], own_sem)
    own_taps.start()
    loads = [
        pltpu.make_async_copy(src, dst, load_sem.at[i])
        for i, (src, dst) in enumerate(
            ((key_hbm, key_ref), (value_hbm, value_ref), (query_hbm, query_ref))
        )
    ]
    for load in loads:
        load.start()
    barrier = pltpu.get_barrier_semaphore()

    @pl.when(has_left)
    def _():
        pl.semaphore_signal(
            barrier, inc=1, device_id={"seq": me - 1}, device_id_type=pl.DeviceIdType.MESH
        )

    @pl.when(has_right)
    def _():
        pl.semaphore_signal(
            barrier, inc=1, device_id={"seq": me + 1}, device_id_type=pl.DeviceIdType.MESH
        )

    source = [sources_ref[w] for w in range(WIN)]
    holders = [owner_ref[k] for k in range(stretches)]
    source_owner = [
        sum(jnp.where(source[w] == k, holders[k], 0) for k in range(stretches)) for w in range(WIN)
    ]
    source_slot = [jnp.int32(0)] * WIN
    slot_stretch = [jnp.int32(0)] * slots
    count = jnp.int32(0)
    for k in range(stretches):
        holder = holders[k]
        for w in range(WIN - 1):
            source_slot[w] += jnp.where((holder == source_owner[w]) & (k < source[w]), 1, 0)
        here = holder == me
        for t in range(slots):
            slot_stretch[t] += jnp.where(here & (count == t), k, 0)
        count += jnp.where(here, 1, 0)
    chunks = octets * SENT

    def is_mine(c):
        w = c % SENT
        holder = sum(jnp.where(w == k, source_owner[k], 0) for k in range(SENT))
        return jnp.full((STRETCH, 128), holder, jnp.int32) == me

    owners = [jnp.full((STRETCH, 128), source_owner[w], jnp.int32) for w in range(WIN)]

    def choose(mask, yes, no):
        return jnp.where(mask, yes.astype(F32), no.astype(F32))

    first = [
        [last - jnp.maximum(slot_stretch[t] - source[w], -1) for w in range(WIN)]
        for t in range(slots)
    ]

    def gated(slot, o):
        at = (slot, slice(None), pl.ds(pl.multiple_of(o * 128, 128), 128))
        return (key_ref[at].astype(F32) * value_ref[at].astype(F32)).astype(BF16)

    own_taps.wait()

    pl.semaphore_wait(barrier, has_left.astype(jnp.int32) + has_right.astype(jnp.int32))

    @pl.when(has_right)
    def _():
        tap_hop(me, 1).start()

    @pl.when(has_left)
    def _():
        tap_hop(me, -1).start()

    loads[0].wait()
    loads[1].wait()

    @pl.loop(0, octets)
    def _(o):
        for w in range(WIN - 1):
            piece = gated(source_slot[w], o)
            right_ref[o * SENT + w] = piece
            left_ref[o * SENT + w] = piece

    right_lag = HOP * me
    left_lag = HOP * (size - 1 - me)
    lag = jnp.maximum(right_lag, left_lag)

    @pl.loop(0, chunks + HOP * (size - 1))
    def _(s):
        far = s // HOP
        turn = (s % HOP == 0) & (far >= 1)

        @pl.when(turn & (me >= far))
        def _():
            tap_hop(me - far, -1).wait_recv()

            @pl.when(has_right)
            def _():
                tap_hop(me - far, 1).start()

        @pl.when(turn & (me + far < size))
        def _():
            tap_hop(me + far, 1).wait_recv()

            @pl.when(has_left)
            def _():
                tap_hop(me + far, -1).start()

        @pl.when((s >= right_lag) & (s < right_lag + chunks))
        def _():
            o = s - right_lag

            @pl.when(has_left)
            def _():
                right_hop(o).wait_recv()
                right_ref[o] = choose(is_mine(o), right_ref[o], from_left_ref[o]).astype(BF16)

            @pl.when(has_right)
            def _():
                @pl.when(o >= AHEAD)
                def _():
                    right_hop(o - AHEAD).wait_send()

                right_hop(o).start()

        @pl.when((s >= left_lag) & (s < left_lag + chunks))
        def _():
            o = s - left_lag

            @pl.when(has_right)
            def _():
                left_hop(o).wait_recv()
                left_ref[o] = choose(is_mine(o), left_ref[o], from_right_ref[o]).astype(BF16)

            @pl.when(has_left)
            def _():
                @pl.when(o >= AHEAD)
                def _():
                    left_hop(o - AHEAD).wait_send()

                left_hop(o).start()

        @pl.when(s == lag)
        def _():
            turn_filters(taps_ref, padded_ref)
            loads[2].wait()

        @pl.when((s >= lag) & (s < lag + chunks) & ((s - lag) % SENT == SENT - 1))
        def _():
            o = (s - lag) // SENT
            spans = padded_ref[pl.ds(pl.multiple_of(o * OCT, OCT), OCT), :]
            for g in range(OCT):
                spread = jnp.broadcast_to(spans[g : g + 1, :], (PIECE, width))
                turned = pltpu.roll(spread, width - 15, 1, stride=1, stride_axis=0).astype(BF16)
                for n in range(stretches + 2):
                    g_ref[g, n] = turned[:, 128 * n : 128 * (n + 1)]

            pieces = []
            for w in range(WIN):
                if w == WIN - 1:
                    rows = gated(slots - 1, o)
                    rows = choose(owners[w] == me, rows, jnp.zeros_like(rows))
                else:
                    rows = choose(owners[w] <= me, right_ref[o * SENT + w], left_ref[o * SENT + w])
                pieces.append(
                    block_transpose([rows[PIECE * e : PIECE * (e + 1), :] for e in range(OCT)])
                )
            results = []
            for g in range(OCT):
                columns = jnp.concatenate(
                    [unrolled_columns(pieces[w][g]) for w in range(WIN)], axis=0
                )
                taps = jnp.concatenate(
                    [
                        jnp.concatenate(
                            [g_ref[g, first[t][w] + half] for w in range(WIN) for half in range(2)],
                            axis=1,
                        )
                        for t in range(slots)
                    ],
                    axis=0,
                )
                results.append(jnp.dot(taps, columns, preferred_element_type=F32))
            lanes = pl.ds(pl.multiple_of(o * 128, 128), 128)
            for t in range(slots):
                rows = block_transpose(
                    [results[g][PIECE * t : PIECE * (t + 1), :] for g in range(OCT)]
                )
                for a in range(OCT):
                    at = (slice(STRETCH * t + PIECE * a, STRETCH * t + PIECE * (a + 1)), lanes)
                    out_ref[at] = (query_ref[at].astype(F32) * rows[a]).astype(BF16)

    for shard in range(size):
        @pl.when(has_right & (me >= shard))
        def _():
            tap_hop(shard, 1).wait_send()

        @pl.when(has_left & (me <= shard))
        def _():
            tap_hop(shard, -1).wait_send()

    @pl.loop(max(chunks - AHEAD, 0), chunks)
    def _(o):
        @pl.when(has_right)
        def _():
            right_hop(o).wait_send()

        @pl.when(has_left)
        def _():
            left_hop(o).wait_send()


def shards(size, key_proj, value_proj, query_proj, filters, sources, owner):
    rows, channels = key_proj.shape
    groups, span = filters.shape
    stretches = owner.shape[0]
    octets = channels // 128
    lags = size * span
    chunks = octets * SENT
    by_slot = (rows // STRETCH, STRETCH, channels)
    key_proj, value_proj = key_proj.reshape(by_slot), value_proj.reshape(by_slot)
    vmem = pl.BlockSpec(memory_space=pltpu.VMEM)
    hbm = pl.BlockSpec(memory_space=pl.ANY)
    smem = pl.BlockSpec(memory_space=pltpu.SMEM)
    chunk = pltpu.VMEM((chunks, STRETCH, 128), BF16)
    dma = pltpu.SemaphoreType.DMA
    return pl.pallas_call(
        functools.partial(fused_kernel, size),
        out_shape=jax.ShapeDtypeStruct((rows, channels), BF16),
        in_specs=[smem, smem, hbm, hbm, hbm, hbm],
        out_specs=vmem,
        scratch_shapes=[
            pltpu.VMEM(by_slot, BF16), pltpu.VMEM(by_slot, BF16), pltpu.VMEM((rows, channels), BF16),
            chunk, chunk, chunk, chunk,
            pltpu.VMEM((size, groups, span), BF16),
            pltpu.VMEM((groups, lags + 256), F32),
            pltpu.VMEM((OCT, stretches + 2, PIECE, 128), BF16),
            dma, dma((3,)), dma((size,)), dma((size,)), dma((size,)),
            dma((chunks,)), dma((chunks,)), dma((chunks,)), dma((chunks,)),
        ],
        compiler_params=pltpu.CompilerParams(
            vmem_limit_bytes=40 * 2**20, collective_id=0, has_side_effects=True
        ),
    )(sources, owner, key_proj, value_proj, query_proj, filters)


def solution(mesh):
    return jax.shard_map(
        functools.partial(shards, mesh.shape["seq"]),
        mesh=mesh,
        in_specs=(
            P(("rep", "seq"), "ch"),
            P(("rep", "seq"), "ch"),
            P(("rep", "seq"), "ch"),
            P("ch", "seq"),
            P("rep"),
            P("rep"),
        ),
        out_specs=P(("rep", "seq"), "ch"),
        check_vma=False,
    )
```
